32 devices in a mesh: seq: 8 (over z, x), head: 4 (over y, core).
Axes of the slice: x: 2, y: 2, z: 4, core: 2. Of those that a mesh axis runs over, the one named last changes fastest.
Arguments:
- queries: float32 [8192, 4096], P('seq', 'head'), may hold values from -6 to 6
- keys: float32 [8192, 4096], P('seq', 'head'), may hold values from -6 to 6
- values: float32 [8192, 4096], P('seq', 'head'), may hold values from -6 to 6
- out_grad: float32 [8192, 4096], P('seq', 'head'), may hold values from -6 to 6
- inputs: float32 [8192, 4096], P('seq', 'head'), may hold values from -20 to 20
- row_state: float32 [4, 4096], P('head', 'seq'), may hold values from 0.2 to 5
- col_state: float32 [8, 4096], P('seq', 'head'), may hold values from 0.2 to 5
Outputs:
- query_grad: float32 [8192, 4096], P('seq', 'head')
- key_grad: float32 [8192, 4096], P('seq', 'head')
- update: float32 [4096, 4096], P('seq', 'head')
- row_next: float32 [4, 4096], P('head', 'seq')
- col_next: float32 [8, 4096], P('seq', 'head')
The draws below stay inside these ranges and needn't reach their ends.
All inputs are finite; a program needn't handle non-finite values.
Results may differ from the reference program's by a relative error of at most 0.0001.
Values sent between devices are 32-bit elements; how exact they have to be, the bound alone decides.
No kernel may reach another device: no remote copies, remote signals or barrier semaphores. Data moves between devices by JAX's collectives and lax.ppermute only.
A program may use at most 128 MiB of HBM per device.

```python
import math
import jax
import jax.numpy as jnp
from jax import lax

HEADS = 32
HEAD_DIM = 128
D = 4096
TOKENS = 8192
OUT_BLK = 512
IN_BLK = 1024
N_SEQ = 8
N_HEAD = 4


def draw_inputs(key, part):
    key_base, key_cols = jax.random.split(jax.random.fold_in(key, 17), 2)
    column_scale = 10.0 ** jax.random.uniform(key_cols, (1, D), jnp.float32, -0.5, 0.5)
    drawn = jax.random.normal(key_base, (TOKENS, D), jnp.float32) * column_scale
    return jnp.clip(drawn, -20.0, 20.0)


def steps_of(stream_key, extent, cuts, low, high):
    loudness, own = 1.0, jax.random.fold_in(stream_key, 6)
    for axis_at, shards_of in cuts:
        heights = jnp.exp(jax.random.uniform(jax.random.fold_in(own, axis_at), (shards_of,), jnp.float32, low / len(cuts), high / len(cuts)))
        loudness = loudness * jnp.repeat(heights, extent[axis_at] // shards_of).reshape([-1 if axis == axis_at else 1 for axis in range(len(extent))])
    return loudness


def gaussian(rng, dims, spread, reach, shards=(), held_as=jnp.bfloat16):
    values = spread * jax.random.normal(rng, dims, jnp.float32)
    if shards:
        values = values * steps_of(rng, dims, shards, -0.22, 0.18)
    return jnp.clip(values, -reach, reach).astype(held_as)


def setup_inputs(seed: int = 0) -> dict:
    streams_of = jax.random.split(jax.random.key(seed), 8)
    return {
        "queries": gaussian(streams_of[0], (TOKENS, D), 1.0, 6.0, ((0, 8), (1, 4)), jnp.float32),
        "keys": gaussian(streams_of[1], (TOKENS, D), 1.0, 6.0, ((0, 8), (1, 4)), jnp.float32),
        "values": gaussian(streams_of[2], (TOKENS, D), 1.0, 6.0, ((0, 8), (1, 4)), jnp.float32),
        "out_grad": gaussian(streams_of[3], (TOKENS, D), 1.0, 6.0, ((0, 8), (1, 4)), jnp.float32),
        "inputs": draw_inputs(jax.random.fold_in(streams_of[7], 71), 0),
        "row_state": jnp.clip(jnp.exp(math.log(5.0) - 3.218876 * jax.random.uniform(streams_of[5], (N_HEAD, D), jnp.float32) ** steps_of(streams_of[5], (N_HEAD, D), ((0, 4), (1, 8)), -0.2, 0.2)), 0.2, 5.0),
        "col_state": jnp.clip(jnp.exp(math.log(5.0) - 3.218876 * jax.random.uniform(streams_of[6], (N_SEQ, D), jnp.float32) ** steps_of(streams_of[6], (N_SEQ, D), ((0, 8), (1, 4)), -0.2, 0.2)), 0.2, 5.0),
    }


highest = lax.Precision.HIGHEST
moment_eps = 1e-06
decay_rate = 0.9

def causal_terms(left_rows, right_rows):
    blk_size = left_rows.shape[0]
    scores = jnp.einsum('thd,shd->hts', left_rows, right_rows, precision=highest)
    rows_idx = lax.broadcasted_iota(jnp.int32, (blk_size, blk_size), 0)
    cols_idx = lax.broadcasted_iota(jnp.int32, (blk_size, blk_size), 1)
    causal_mask = (cols_idx <= rows_idx).astype(jnp.float32)
    return scores * causal_mask[None]

def reference(queries, keys, values, out_grad, inputs, row_state, col_state):
    blk_size = min(512, TOKENS)
    num_blocks = TOKENS // blk_size
    attn_scale = 1.0 / jnp.sqrt(jnp.float32(HEAD_DIM * TOKENS))

    def split_blocks(array):
        return array.reshape(num_blocks, blk_size, HEADS, HEAD_DIM)
    query_blocks = split_blocks(queries)
    key_blocks = split_blocks(keys)
    value_blocks = split_blocks(values)
    grad_blocks = split_blocks(out_grad)

    def forward_step(state_sum, pieces):
        query_part, key_part, value_part, grad_part = pieces
        grad_value = causal_terms(grad_part, value_part)
        inner = jnp.einsum('hts,shd->thd', grad_value, key_part, precision=highest)
        carried = jnp.einsum('tha,hab->thb', grad_part, state_sum, precision=highest)
        new_state = state_sum + jnp.einsum('sha,shb->hab', value_part, key_part, precision=highest)
        return (new_state, attn_scale * (inner + carried))

    def reverse_step(state_sum, pieces):
        query_part, key_part, value_part, grad_part = pieces
        grad_value = causal_terms(grad_part, value_part)
        query_key = causal_terms(query_part, key_part)
        inner_key = jnp.einsum('hts,thd->shd', grad_value, query_part, precision=highest)
        inner_value = jnp.einsum('hts,thd->shd', query_key, grad_part, precision=highest)
        carried_key = jnp.einsum('shb,hab->sha', value_part, state_sum, precision=highest)
        carried_value = jnp.einsum('sha,hab->shb', key_part, state_sum, precision=highest)
        new_state = state_sum + jnp.einsum('tha,thb->hab', query_part, grad_part, precision=highest)
        return (new_state, (attn_scale * (inner_key + carried_key), attn_scale * (inner_value + carried_value)))
    zero_state = jnp.zeros((HEADS, HEAD_DIM, HEAD_DIM), jnp.float32)
    pieces = (query_blocks, key_blocks, value_blocks, grad_blocks)
    final_fwd, query_grad = lax.scan(forward_step, zero_state, pieces)
    final_rev, (key_grad, value_grad) = lax.scan(reverse_step, zero_state, pieces, reverse=True)
    query_grad = query_grad.reshape(TOKENS, D)
    key_grad = key_grad.reshape(TOKENS, D)
    value_grad = value_grad.reshape(TOKENS, D)
    weight_grad = jnp.dot(value_grad.T, inputs, precision=highest, preferred_element_type=jnp.float32)
    weight_grad = weight_grad / jnp.sqrt(jnp.float32(TOKENS))
    grad_tiles = weight_grad.reshape(N_SEQ, OUT_BLK, N_HEAD, IN_BLK)
    squares = grad_tiles * grad_tiles + moment_eps
    row_mean = jnp.transpose(lax.optimization_barrier(jnp.mean(squares, axis=3)), (2, 0, 1)).reshape(N_HEAD, D)
    col_mean = lax.optimization_barrier(jnp.mean(squares, axis=1)).reshape(N_SEQ, D)
    row_next = decay_rate * row_state + (1.0 - decay_rate) * row_mean
    col_next = decay_rate * col_state + (1.0 - decay_rate) * col_mean
    row_tiles = jnp.transpose(row_next.reshape(N_HEAD, N_SEQ, OUT_BLK), (1, 2, 0))
    row_average = lax.optimization_barrier(jnp.mean(row_tiles, axis=1, keepdims=True))
    col_tiles = col_next.reshape(N_SEQ, N_HEAD, IN_BLK)[:, None, :, :]
    second = row_tiles[:, :, :, None] * col_tiles / row_average[:, :, :, None]
    update = (grad_tiles / jnp.sqrt(second)).reshape(D, D)
    return (query_grad, key_grad, update, row_next, col_next)
```

```python
import functools
import jax
import jax.numpy as jnp
from jax import lax
from jax.experimental import pallas as pl
from jax.experimental.pallas import tpu as pltpu
from jax.sharding import PartitionSpec as P

HEAD_DIM = 128
MOMENT_EPS = 1e-06
DECAY = 0.9
F32 = jnp.float32
BF16 = jnp.bfloat16
AXES = ("seq", "head")
NN = (((1,), (0,)), ((), ()))
NT = (((1,), (1,)), ((), ()))
TN = (((0,), (0,)), ((), ()))


def split(x):
    hi = x.astype(BF16)
    return hi, (x - hi.astype(F32)).astype(BF16)


def dot3(a, b, dims):
    mul = functools.partial(lax.dot_general, dimension_numbers=dims, preferred_element_type=F32)
    return mul(a[0], b[0]) + (mul(a[0], b[1]) + mul(a[1], b[0]))


def params(mib=48):
    return pltpu.CompilerParams(vmem_limit_bytes=mib * 2**20)


def cost(flops, nbytes):
    return pl.CostEstimate(flops=int(flops), bytes_accessed=int(nbytes), transcendentals=0)


def outer_body(left, right, out):
    out[0] = dot3(split(left[...]), split(right[...]), TN)


def outer_sums(left, right, heads_of, count):
    tokens = left.shape[0]
    spec = pl.BlockSpec((tokens, HEAD_DIM), lambda j: (0, heads_of(j)))
    return pl.pallas_call(
        outer_body,
        grid=(count,),
        in_specs=[spec, spec],
        out_specs=pl.BlockSpec((1, HEAD_DIM, HEAD_DIM), lambda j: (j, 0, 0)),
        out_shape=jax.ShapeDtypeStruct((count, HEAD_DIM, HEAD_DIM), F32),
        compiler_params=params(),
        cost_estimate=cost(6 * count * tokens * HEAD_DIM**2, 8 * count * tokens * HEAD_DIM),
        name="outer_sums",
    )(left, right)


def value_body(scale, blk, q, k, g, state, out):
    count = q.shape[0] // blk
    later = state[0]
    src = lax.broadcasted_iota(jnp.int32, (blk, blk), 0)
    tgt = lax.broadcasted_iota(jnp.int32, (blk, blk), 1)
    for n in reversed(range(count)):
        rows = pl.ds(n * blk, blk)
        qn, kn, gn = split(q[rows, :]), split(k[rows, :]), split(g[rows, :])
        scores = jnp.where(src <= tgt, dot3(kn, qn, NT), 0.0)
        grad = dot3(split(scores), gn, NN) + dot3(kn, split(later), NN)
        out[0, :, rows] = (scale * grad).T
        if n:
            later = later + dot3(qn, gn, TN)


def value_grads(q, k, g, state, scale, heads_of):
    tokens, count = q.shape[0], state.shape[0]
    blk = min(256, tokens)
    spec = pl.BlockSpec((tokens, HEAD_DIM), lambda j: (0, heads_of(j)))
    return pl.pallas_call(
        functools.partial(value_body, scale, blk),
        grid=(count,),
        in_specs=[spec, spec, spec, pl.BlockSpec((1, HEAD_DIM, HEAD_DIM), lambda j: (j, 0, 0))],
        out_specs=pl.BlockSpec((1, HEAD_DIM, tokens), lambda j: (j, 0, 0)),
        out_shape=jax.ShapeDtypeStruct((count, HEAD_DIM, tokens), F32),
        compiler_params=params(),
        cost_estimate=cost(12 * count * tokens * blk * HEAD_DIM, 16 * count * tokens * HEAD_DIM),
        name="value_grads",
    )(q, k, g, state)


def query_key_body(scale, blk, q, k, v, g, fwd, rev, qg, kg):
    count = q.shape[0] // blk
    tgt = lax.broadcasted_iota(jnp.int32, (blk, blk), 0)
    src = lax.broadcasted_iota(jnp.int32, (blk, blk), 1)
    before = [fwd[0]]
    for n in range(count - 1):
        rows = pl.ds(n * blk, blk)
        before.append(before[-1] + dot3(split(v[rows, :]), split(k[rows, :]), TN))
    later = rev[0, 0]
    for n in reversed(range(count)):
        rows = pl.ds(n * blk, blk)
        qn, kn = split(q[rows, :]), split(k[rows, :])
        vn, gn = split(v[rows, :]), split(g[rows, :])
        scores = split(jnp.where(src <= tgt, dot3(gn, vn, NT), 0.0))
        qg[rows, :] = scale * (dot3(scores, kn, NN) + dot3(gn, split(before[n]), NN))
        kg[rows, :] = scale * (dot3(scores, qn, TN) + dot3(vn, split(later), NT))
        if n:
            later = later + dot3(qn, gn, TN)


def query_key_grads(q, k, v, g, fwd, rev, scale):
    tokens, width = q.shape
    heads, chunks = width // HEAD_DIM, rev.shape[0]
    blk = min(256, tokens)
    spec = pl.BlockSpec((tokens, HEAD_DIM), lambda n: (0, n))
    return pl.pallas_call(
        functools.partial(query_key_body, scale, blk),
        grid=(heads,),
        in_specs=[spec] * 4
        + [
            pl.BlockSpec((1, HEAD_DIM, HEAD_DIM), lambda n: (n, 0, 0)),
            pl.BlockSpec((1, 1, HEAD_DIM, HEAD_DIM), lambda n: (n % chunks, n // chunks, 0, 0)),
        ],
        out_specs=[spec, spec],
        out_shape=[jax.ShapeDtypeStruct((tokens, width), F32)] * 2,
        compiler_params=params(),
        cost_estimate=cost(30 * tokens * blk * width, 24 * tokens * width),
        name="query_key_grads",
    )(q, k, v, g, fwd, rev)


def order_body(scal, own, partner, mine_hi, mine_lo, other_hi, other_lo):
    first = scal[0] == 1
    a, b = own[...], partner[...]
    mine_hi[...], mine_lo[...] = split(jnp.where(first, a, b))
    other_hi[...], other_lo[...] = split(jnp.where(first, b, a))


def order_inputs(scal, own, partner, at):
    tokens, width = partner.shape
    blk = min(256, tokens)
    spec = pl.BlockSpec((blk, width), lambda n, s: (n, 0))
    return pl.pallas_call(
        order_body,
        grid_spec=pltpu.PrefetchScalarGridSpec(
            num_scalar_prefetch=1,
            grid=(tokens // blk,),
            in_specs=[pl.BlockSpec((blk, width), lambda n, s: (n, at)), spec],
            out_specs=[spec] * 4,
        ),
        out_shape=[jax.ShapeDtypeStruct((tokens, width), BF16)] * 4,
        compiler_params=params(),
        cost_estimate=cost(8 * tokens * width, 16 * tokens * width),
        name="order_inputs",
    )(scal, own, partner)


def weight_body(ny, low, scal, *refs):
    mine, other = refs[:ny], refs[ny : 2 * ny]
    mine_hi, mine_lo, other_hi, other_lo = refs[2 * ny : 2 * ny + 4]
    outs = refs[2 * ny + 4 :]
    for jj in reversed(range(low)):
        j = scal[1] ^ jj
        total = None
        for group, hi, lo in ((mine, mine_hi, mine_lo), (other, other_hi, other_lo)):
            parts = [split(ref[j]) for ref in group]
            high = jnp.concatenate([p[0] for p in parts], axis=0)
            both = jnp.concatenate([high] + [p[1] for p in parts], axis=0)
            wide = jnp.dot(both, hi[...], preferred_element_type=F32)
            rows = high.shape[0]
            term = wide[:rows] + (wide[rows:] + jnp.dot(high, lo[...], preferred_element_type=F32))
            total = term if total is None else total + term
        height = total.shape[0] // ny
        for i in range(ny):
            outs[jj][scal[2] ^ i] = total[i * height : (i + 1) * height]


def weight_parts(scal, mine, other, terms):
    ny = len(mine)
    low, height, tokens = mine[0].shape
    width = terms[0].shape[1]
    blk = min(256, width)
    grad_spec = pl.BlockSpec((low, height, tokens), lambda n, s: (0, 0, 0))
    term_spec = pl.BlockSpec((tokens, blk), lambda n, s: (0, n))
    return pl.pallas_call(
        functools.partial(weight_body, ny, low),
        grid_spec=pltpu.PrefetchScalarGridSpec(
            num_scalar_prefetch=1,
            grid=(width // blk,),
            in_specs=[grad_spec] * (2 * ny) + [term_spec] * 4,
            out_specs=[pl.BlockSpec((ny, height, blk), lambda n, s: (0, 0, n))] * low,
        ),
        out_shape=[jax.ShapeDtypeStruct((ny, height, width), F32)] * low,
        compiler_params=params(),
        cost_estimate=cost(
            12 * ny * low * height * tokens * width,
            8 * ny * low * height * tokens + 8 * tokens * width + 4 * ny * low * height * width,
        ),
        name="weight_parts",
    )(scal, *mine, *other, *terms)


def update_body(scale, chunks, halves, terms, row_state, col_state, *refs):
    parts, (update, row_next, col_next) = refs[: chunks * halves * terms], refs[chunks * halves * terms :]
    height, width = parts[0].shape[-2:]
    rows, columns = chunks * height, halves * width
    col_sums = [jnp.zeros((1, width), F32)] * halves
    row_cols = []
    total = jnp.zeros((1, 1), F32)
    for a in range(chunks):
        row_sum = jnp.zeros((height, 1), F32)
        for c in range(halves):
            at = (a * halves + c) * terms
            block = parts[at][0]
            for ref in parts[at + 1 : at + terms]:
                block = block + ref[0]
            block = block * scale
            update[pl.ds(a * height, height), pl.ds(c * width, width)] = block
            squares = block * block
            row_sum = row_sum + jnp.sum(squares, axis=1, keepdims=True)
            col_sums[c] = col_sums[c] + jnp.sum(squares, axis=0, keepdims=True)
        mean = row_sum * (1.0 / columns) + MOMENT_EPS
        lanes = jnp.broadcast_to(mean, (height, height)).T[:1]
        nxt = DECAY * row_state[:, pl.ds(a * height, height)] + (1.0 - DECAY) * lanes
        row_next[:, pl.ds(a * height, height)] = nxt
        total = total + jnp.sum(nxt, axis=1, keepdims=True)
        row_cols.append(jnp.broadcast_to(nxt, (height, height)).T[:, :1])
    average = total * (1.0 / rows)
    for c in range(halves):
        cols = pl.ds(c * width, width)
        nxt = DECAY * col_state[:, cols] + (1.0 - DECAY) * (col_sums[c] * (1.0 / rows) + MOMENT_EPS)
        col_next[:, cols] = nxt
        for a in range(chunks):
            at = (pl.ds(a * height, height), cols)
            update[at] = update[at] / jnp.sqrt(row_cols[a] * nxt / average)


def update_block(parts, row_state, col_state, scale):
    chunks, halves, terms = len(parts), len(parts[0]), len(parts[0][0])
    flat = [x for row in parts for cell in row for x in cell]
    height, width = flat[0].shape[-2:]
    whole = pl.BlockSpec(memory_space=pltpu.VMEM)
    cell = pl.BlockSpec((1, height, width), lambda n: (0, 0, 0))
    full = lambda x: pl.BlockSpec(x.shape, lambda n: (0, 0))
    shape = (chunks * height, halves * width)
    out_shape = [
        jax.ShapeDtypeStruct(shape, F32),
        jax.ShapeDtypeStruct(row_state.shape, F32),
        jax.ShapeDtypeStruct(col_state.shape, F32),
    ]
    return pl.pallas_call(
        functools.partial(update_body, scale, chunks, halves, terms),
        grid=(1,),
        in_specs=[full(row_state), full(col_state)] + [cell] * len(flat),
        out_specs=[full(x) for x in out_shape],
        out_shape=out_shape,
        compiler_params=params(),
        cost_estimate=cost(20 * shape[0] * shape[1], 16 * shape[0] * shape[1]),
        name="update_block",
    )(row_state, col_state, *flat)


def shards(queries, keys, values, out_grad, inputs, row_state, col_state):
    tokens, width = queries.shape
    n_seq, n_head = lax.axis_size("seq"), lax.axis_size("head")
    heads = width // HEAD_DIM
    low = n_seq // n_head
    ny = n_head // 2
    chunks = heads // low
    halves = 2
    scale = 1.0 / float(HEAD_DIM * tokens * n_seq) ** 0.5
    weight_scale = 1.0 / float(tokens * n_seq) ** 0.5

    def permute(x, go):
        pairs = [
            (s * n_head + h, (lambda d: d[0] * n_head + d[1])(go(s, h)))
            for s in range(n_seq)
            for h in range(n_head)
        ]
        return lax.ppermute(x, AXES, pairs)

    def over_seq(x, bit):
        return permute(x, lambda s, h: (s ^ bit, h))

    def over_head(x, bit):
        return permute(x, lambda s, h: (s, h ^ bit))

    seq, head = lax.axis_index("seq"), lax.axis_index("head")
    plane = (seq // low) & 1
    first = (plane == (head & 1)).astype(jnp.int32)
    scal = jnp.stack([first, seq % low, (head // 2) ^ (seq // (2 * low))]).astype(jnp.int32)

    bits = [1 << n for n in range(n_seq.bit_length() - 1)]

    def scan_states(local, reverse):
        total, enter = local, jnp.zeros_like(local)
        for bit in bits:
            got = over_seq(total, bit)
            take = ((seq & bit) == 0) if reverse else ((seq & bit) != 0)
            enter = enter + jnp.where(take, got, 0.0)
            if bit != bits[-1]:
                total = total + got
        return enter

    half = inputs.shape[1] // halves
    partner = [over_seq(inputs[:, c * half : (c + 1) * half], low) for c in range(halves)]

    def heads_of(a):
        return lambda j: j * chunks + a

    enter_rev = []
    for a in range(chunks):
        local = outer_sums(queries, out_grad, heads_of(a), low)
        enter_rev.append(scan_states(local, True))

    gathered = []
    for a in range(chunks):
        grads = value_grads(queries, keys, out_grad, enter_rev[a], scale, heads_of(a))
        mine = [
            permute(
                grads,
                lambda s, h: (s, h) if ((s // low) & 1) == (h & 1) else (s ^ low, h ^ 1),
            )
        ]
        bit = 1
        while bit < ny:
            mine = mine + [over_head(x, 2 * bit) for x in mine]
            bit *= 2
        gathered.append((mine, [over_head(x, 1) for x in mine]))

    terms = [order_inputs(scal, inputs, partner[c], c) for c in range(halves)]

    cells = []
    for a in range(chunks):
        row = []
        for c in range(halves):
            outs = weight_parts(scal, gathered[a][0], gathered[a][1], terms[c])
            count = low
            while count > 1:
                count //= 2
                got = [over_seq(x, count) for x in outs[count:]]
                outs = [x + y for x, y in zip(outs[:count], got)]
            keep, count = outs[0], ny
            added = [keep]
            while count > 1:
                count //= 2
                got = over_seq(keep[count:], 2 * low * count)
                if count == 1:
                    added = [keep[:1], got]
                else:
                    keep = keep[:count] + got
            row.append(added)
        cells.append(row)

    enter_fwd = scan_states(outer_sums(values, keys, lambda n: n, heads), False)
    query_grad, key_grad = query_key_grads(
        queries, keys, values, out_grad, enter_fwd, jnp.stack(enter_rev), scale
    )
    update, row_next, col_next = update_block(cells, row_state, col_state, weight_scale)
    return (query_grad, key_grad, update, row_next, col_next)


def solution(mesh):
    tok, rows = P("seq", "head"), P("head", "seq")
    return jax.shard_map(
        shards,
        mesh=mesh,
        in_specs=(tok, tok, tok, tok, tok, rows, tok),
        out_specs=(tok, tok, tok, rows, tok),
        check_vma=False,
    )
```

```python
import functools
import jax
import jax.numpy as jnp
from jax import lax
from jax.experimental import pallas as pl
from jax.experimental.pallas import tpu as pltpu
from jax.sharding import PartitionSpec as P


HEAD_DIM = 128
MOMENT_EPS = 1e-06
DECAY = 0.9
F32 = jnp.float32
BF16 = jnp.bfloat16
AXES = ("seq", "head")
ALONE = 1
PIECES = ((2, 2), (2, 2))
SPLIT = (0, 1, 2, 3)
NN = (((1,), (0,)), ((), ()))
NT = (((1,), (1,)), ((), ()))
TN = (((0,), (0,)), ((), ()))


def split(x):
    hi = x.astype(BF16)
    return hi, (x - hi.astype(F32)).astype(BF16)


def times(a, b, dims):
    return lax.dot_general(a, b, dimension_numbers=dims, preferred_element_type=F32)


def mul_nn(a, b):
    wide = jnp.concatenate(b, axis=1)
    columns = b[0].shape[1]
    if a[0].shape[1] == HEAD_DIM:
        low = jnp.concatenate([b[0], jnp.zeros_like(b[0])], axis=1)
        out = times(jnp.concatenate(a, axis=1), jnp.concatenate([wide, low], axis=0), NN)
        return out[:, :columns] + out[:, columns:]
    out = times(a[0], wide, NN)
    return out[:, :columns] + (out[:, columns:] + times(a[1], b[0], NN))


def mul_nt(a, b):
    both = times(jnp.concatenate(a, axis=1), jnp.concatenate([b[0], b[0]], axis=1), NT)
    return both + times(a[0], b[1], NT)


def mul_tn(a, b):
    columns = b[0].shape[1]
    out = times(a[0], jnp.concatenate(b, axis=1), TN)
    return out[:, :columns] + (out[:, columns:] + times(a[1], b[0], TN))


def params(mib=24):
    return pltpu.CompilerParams(vmem_limit_bytes=mib * 2**20)


def cost(flops, nbytes):
    return pl.CostEstimate(flops=int(flops), bytes_accessed=int(nbytes), transcendentals=0)


def by_phase(phase, count):
    return lambda p, n: jnp.where(p == phase, n, jnp.where(p < phase, 0, count - 1))


def outer_body(low, scal, left, right, *outs):
    out = mul_tn(split(left[...]), split(right[...]))
    for jj in range(low):

        @pl.when(pl.program_id(0) == low - 1 - jj)
        def _():
            outs[jj][0] = out


def outer_sums(scal, left, right, low, chunks, begin, count):
    tokens = left.shape[0]
    spec = pl.BlockSpec(
        (tokens, HEAD_DIM), lambda p, n, s: (0, (s[1] ^ (low - 1 - p)) * chunks + begin + n)
    )

    def out_spec(jj):
        at = by_phase(low - 1 - jj, count)
        return pl.BlockSpec((1, HEAD_DIM, HEAD_DIM), lambda p, n, s: (at(p, n), 0, 0))

    return pl.pallas_call(
        functools.partial(outer_body, low),
        grid_spec=pltpu.PrefetchScalarGridSpec(
            num_scalar_prefetch=1,
            grid=(low, count),
            in_specs=[spec, spec],
            out_specs=[out_spec(jj) for jj in range(low)],
        ),
        out_shape=[jax.ShapeDtypeStruct((count, HEAD_DIM, HEAD_DIM), F32)] * low,
        compiler_params=params(),
        cost_estimate=cost(6 * low * count * tokens * HEAD_DIM**2, 8 * low * count * tokens * HEAD_DIM),
        name="outer_sums",
    )(scal, left, right)


def value_body(scale, blk, scal, q, k, g, mine, other, out):
    count = q.shape[0] // blk
    src = lax.broadcasted_iota(jnp.int32, (blk, blk), 0)
    tgt = lax.broadcasted_iota(jnp.int32, (blk, blk), 1)
    later = jnp.where(pl.program_id(0) == 0, mine[0], other[0])
    for n in reversed(range(count)):
        rows = pl.ds(n * blk, blk)
        qn, kn, gn = split(q[rows, :]), split(k[rows, :]), split(g[rows, :])
        scores = jnp.where(src <= tgt, mul_nt(kn, qn), 0.0)
        grad = mul_nn(split(scores), gn) + mul_nn(kn, split(later))
        out[0, :, rows] = (scale * grad).T
        if n:
            later = later + mul_tn(qn, gn)


def value_grads(scal, q, k, g, state, at, scale, low, chunks, a):
    tokens = q.shape[0]
    blk = min(256, tokens)
    spec = pl.BlockSpec((tokens, HEAD_DIM), lambda j, s: (0, (s[1] ^ j) * chunks + a))
    state_spec = pl.BlockSpec((1, HEAD_DIM, HEAD_DIM), lambda j, s: (at, 0, 0))
    return pl.pallas_call(
        functools.partial(value_body, scale, blk),
        grid_spec=pltpu.PrefetchScalarGridSpec(
            num_scalar_prefetch=1,
            grid=(low,),
            in_specs=[spec, spec, spec, state_spec, state_spec],
            out_specs=pl.BlockSpec((1, HEAD_DIM, tokens), lambda j, s: (s[1] ^ j, 0, 0)),
        ),
        out_shape=jax.ShapeDtypeStruct((low, HEAD_DIM, tokens), F32),
        compiler_params=params(),
        cost_estimate=cost(12 * low * tokens * blk * HEAD_DIM, 16 * low * tokens * HEAD_DIM),
        name="value_grads",
    )(scal, q, k, g, *state)


def query_key_body(scale, blk, scal, q, k, v, g, fwd, fwd_other, rev, rev_other, *refs):
    qg, kg = refs[-2:]
    count = q.shape[0] // blk
    here = pl.program_id(0) == 0
    tgt = lax.broadcasted_iota(jnp.int32, (blk, blk), 0)
    src = lax.broadcasted_iota(jnp.int32, (blk, blk), 1)
    before = [jnp.where(here, fwd[0], fwd_other[0])]
    for n in range(count - 1):
        rows = pl.ds(n * blk, blk)
        before.append(before[-1] + mul_tn(split(v[rows, :]), split(k[rows, :])))
    later = jnp.where(here, rev[0], rev_other[0])
    for n in reversed(range(count)):
        rows = pl.ds(n * blk, blk)
        qn, kn = split(q[rows, :]), split(k[rows, :])
        vn, gn = split(v[rows, :]), split(g[rows, :])
        scores = split(jnp.where(src <= tgt, mul_nt(gn, vn), 0.0))
        qg[rows, :] = scale * (mul_nn(scores, kn) + mul_nn(gn, split(before[n])))
        kg[rows, :] = scale * (mul_tn(scores, qn) + mul_nn(vn, split(later.T)))
        if n:
            later = later + mul_tn(qn, gn)


def query_key_grads(scal, q, k, v, g, fwd, rev, at, scale, low, chunks, a, count, filled):
    tokens, width = q.shape
    blk = min(256, tokens)
    spec = pl.BlockSpec((tokens, HEAD_DIM), lambda j, n, s: (0, (s[1] ^ j) * chunks + a + n))
    fwd_spec = pl.BlockSpec((1, HEAD_DIM, HEAD_DIM), lambda j, n, s: (a + n, 0, 0))
    rev_spec = pl.BlockSpec((1, HEAD_DIM, HEAD_DIM), lambda j, n, s: (at + n, 0, 0))
    kept = [pl.BlockSpec(memory_space=pl.ANY)] * len(filled)
    return pl.pallas_call(
        functools.partial(query_key_body, scale, blk),
        grid_spec=pltpu.PrefetchScalarGridSpec(
            num_scalar_prefetch=1,
            grid=(low, count),
            in_specs=[spec] * 4 + [fwd_spec] * 2 + [rev_spec] * 2 + kept,
            out_specs=[spec, spec],
        ),
        out_shape=[jax.ShapeDtypeStruct((tokens, width), F32)] * 2,
        input_output_aliases={9 + n: n for n in range(len(filled))},
        compiler_params=params(),
        cost_estimate=cost(30 * tokens * blk * low * count * HEAD_DIM, 24 * tokens * low * count * HEAD_DIM),
        name="query_key_grads",
    )(scal, q, k, v, g, *fwd, *rev, *filled)


def terms_body(*refs):
    pieces, (hi, lo) = refs[:-2], refs[-2:]
    at = 0
    for ref in pieces:
        cols = pl.ds(at, ref.shape[1])
        hi[:, cols], lo[:, cols] = split(ref[...])
        at += ref.shape[1]


def split_terms(pieces):
    tokens, width = pieces[0].shape[0], sum(x.shape[1] for x in pieces)
    blk = min(256, tokens)
    spec = pl.BlockSpec((blk, width), lambda n: (n, 0))
    return pl.pallas_call(
        terms_body,
        grid=(tokens // blk,),
        in_specs=[pl.BlockSpec((blk, x.shape[1]), lambda n: (n, 0)) for x in pieces],
        out_specs=[spec] * 2,
        out_shape=[jax.ShapeDtypeStruct((tokens, width), BF16)] * 2,
        compiler_params=params(),
        cost_estimate=cost(4 * tokens * width, 8 * tokens * width),
        name="split_terms",
    )(*pieces)


def rows_times(blocks, hi, lo):
    parts = [split(x) for x in blocks]
    high = jnp.concatenate([p[0] for p in parts], axis=0)
    both = jnp.concatenate([high] + [p[1] for p in parts], axis=0)
    wide = jnp.dot(both, hi, preferred_element_type=F32)
    rows = high.shape[0]
    return wide[:rows] + (wide[rows:] + jnp.dot(high, lo, preferred_element_type=F32))


def weight_body(ny, low, counts, scal, *refs):
    mine, other = refs[:ny], refs[ny : 2 * ny]
    own_hi, own_lo = refs[2 * ny : 2 * ny + 2]
    far, outs = refs[2 * ny + 2 : -low], refs[-low:]
    first = scal[0] == 1
    a, b = [x[0] for x in mine], [x[0] for x in other]
    if far:
        far_hi, far_lo, at = far[0][...], far[1][...], 0
        for c in range(1, len(counts)):
            at += counts[c - 1]
            later = pl.program_id(1) >= at
            far_hi = jnp.where(later, far[2 * c][...], far_hi)
            far_lo = jnp.where(later, far[2 * c + 1][...], far_lo)
        own_rows = [jnp.where(first, x, y) for x, y in zip(a, b)]
        far_rows = [jnp.where(first, y, x) for x, y in zip(a, b)]
        total = rows_times(own_rows, own_hi[...], own_lo[...]) + rows_times(far_rows, far_hi, far_lo)
        places = [(scal[2] ^ n,) for n in range(ny)]
    else:
        total = rows_times(a + b, own_hi[...], own_lo[...])
        places = [(1 - scal[0], scal[2] ^ n) for n in range(ny)]
        places += [(scal[0], scal[2] ^ n) for n in range(ny)]
    height = total.shape[0] // len(places)
    for jj in range(low):

        @pl.when(pl.program_id(0) == low - 1 - jj)
        def _():
            for n, place in enumerate(places):
                outs[jj][place] = total[n * height : (n + 1) * height]


def weight_parts(scal, mine, other, own, fars, offset, width):
    ny = len(mine)
    low, height, tokens = mine[0].shape
    widths = [x[0].shape[1] for x in fars] or [width]
    blk = 256 if all(x % 256 == 0 for x in widths + [offset]) else 128
    counts = [x // blk for x in widths]
    count, first = width // blk, offset // blk
    lead = (ny, height) if fars else (2, ny, height)
    grad_spec = pl.BlockSpec((1, height, tokens), lambda p, n, s: (s[1] ^ (low - 1 - p), 0, 0))
    own_spec = pl.BlockSpec((tokens, blk), lambda p, n, s: (0, n + first))

    def far_spec(c):
        begin = sum(counts[:c])
        return pl.BlockSpec((tokens, blk), lambda p, n, s: (0, jnp.clip(n - begin, 0, counts[c] - 1)))

    def out_spec(jj):
        col = by_phase(low - 1 - jj, count)
        zeros = (0,) * len(lead)
        return pl.BlockSpec(lead + (blk,), lambda p, n, s: zeros + (col(p, n),))

    return pl.pallas_call(
        functools.partial(weight_body, ny, low, counts),
        grid_spec=pltpu.PrefetchScalarGridSpec(
            num_scalar_prefetch=1,
            grid=(low, count),
            in_specs=[grad_spec] * (2 * ny)
            + [own_spec] * 2
            + [far_spec(c) for c in range(len(fars)) for _ in range(2)],
            out_specs=[out_spec(jj) for jj in range(low)],
        ),
        out_shape=[jax.ShapeDtypeStruct(lead + (width,), F32)] * low,
        compiler_params=params(),
        cost_estimate=cost(
            12 * ny * low * height * tokens * width,
            8 * ny * low * height * tokens + 8 * tokens * width + 8 * ny * height * width,
        ),
        name="weight_parts",
    )(scal, *mine, *other, *own, *[x for pair in fars for x in pair])


def update_body(scale, counts, row_state, col_state, *refs):
    parts, (update, row_next, col_next) = list(refs[:-3]), refs[-3:]
    height = parts[0].shape[-2]
    rows, columns = update.shape
    row_cols = []
    total = jnp.zeros((1, 1), F32)
    col_next[...] = jnp.zeros_like(col_next)
    for a, cells in enumerate(counts):
        at = pl.ds(a * height, height)
        row_sum, begin = jnp.zeros((height, 1), F32), 0
        for count in cells:
            cols = pl.ds(begin, parts[0].shape[-1])
            begin += parts[0].shape[-1]
            block = parts.pop(0)[0]
            for _ in range(count - 1):
                block = block + parts.pop(0)[0]
            block = block * scale
            update[at, cols] = block
            squares = block * block
            row_sum = row_sum + jnp.sum(squares, axis=1, keepdims=True)
            col_next[:, cols] += jnp.sum(squares, axis=0, keepdims=True)
        mean = row_sum * (1.0 / columns) + MOMENT_EPS
        lanes = jnp.broadcast_to(mean, (height, height)).T[:1]
        nxt = DECAY * row_state[:, at] + (1.0 - DECAY) * lanes
        row_next[:, at] = nxt
        total = total + jnp.sum(nxt, axis=1, keepdims=True)
        row_cols.append(jnp.broadcast_to(nxt, (height, height)).T[:, :1])
    average = total * (1.0 / rows)
    nxt = DECAY * col_state[...] + (1.0 - DECAY) * (col_next[...] * (1.0 / rows) + MOMENT_EPS)
    col_next[...] = nxt
    for a in range(len(counts)):
        at = pl.ds(a * height, height)
        update[at, :] = update[at, :] / jnp.sqrt(row_cols[a] * nxt / average)


def update_block(parts, row_state, col_state, scale):
    chunks = len(parts)
    counts = tuple(tuple(len(cell) for cell in row) for row in parts)
    flat = [x for row in parts for cell in row for x in cell]
    height = flat[0].shape[-2]
    cell = lambda x: pl.BlockSpec((1,) + x.shape[-2:], lambda n: (0, 0, 0))
    full = lambda x: pl.BlockSpec(x.shape, lambda n: (0, 0))
    shape = (chunks * height, col_state.shape[1])
    out_shape = [
        jax.ShapeDtypeStruct(shape, F32),
        jax.ShapeDtypeStruct(row_state.shape, F32),
        jax.ShapeDtypeStruct(col_state.shape, F32),
    ]
    return pl.pallas_call(
        functools.partial(update_body, scale, counts),
        grid=(1,),
        in_specs=[full(row_state), full(col_state)] + [cell(x) for x in flat],
        out_specs=[full(x) for x in out_shape],
        out_shape=out_shape,
        compiler_params=params(),
        cost_estimate=cost(20 * shape[0] * shape[1], 16 * shape[0] * shape[1]),
        name="update_block",
    )(row_state, col_state, *flat)


def shards(queries, keys, values, out_grad, inputs, row_state, col_state):
    tokens, width = queries.shape
    n_seq, n_head = lax.axis_size("seq"), lax.axis_size("head")
    heads = width // HEAD_DIM
    low = n_seq // n_head
    ny = n_head // 2
    chunks = heads // low
    scale = 1.0 / float(HEAD_DIM * tokens * n_seq) ** 0.5
    weight_scale = 1.0 / float(tokens * n_seq) ** 0.5
    assert low == 2 and chunks > 1

    def permute(x, go):
        pairs = []
        for s in range(n_seq):
            for h in range(n_head):
                to = go(s, h)
                if to is not None:
                    pairs.append((s * n_head + h, to[0] * n_head + to[1]))
        return lax.ppermute(x, AXES, pairs)

    def over_seq(x, bit):
        return permute(x, lambda s, h: (s ^ bit, h))

    def over_head(x, bit):
        return permute(x, lambda s, h: (s, h ^ bit))

    seq, head = lax.axis_index("seq"), lax.axis_index("head")
    plane = (seq // low) & 1
    first = plane == (head & 1)
    part = seq % low
    scal = jnp.stack([first.astype(jnp.int32), part, (head // 2) ^ (seq // (2 * low))]).astype(jnp.int32)

    def scan_states(sums, reverse):
        keep, send = sums
        got = over_seq(send, 1)
        total, enter, bit = keep + got, jnp.zeros_like(keep), low
        while bit < n_seq:
            came = over_seq(total, bit)
            take = ((seq & bit) == 0) if reverse else ((seq & bit) != 0)
            enter = enter + jnp.where(take, came, 0.0)
            bit *= 2
            if bit < n_seq:
                total = total + came
        last = 0 if reverse else 1
        mine = enter + jnp.where(part == last, got, 0.0)
        out = enter + jnp.where(part == last, 0.0, keep)
        return mine, over_seq(out, 1)

    sums = outer_sums(scal, queries, out_grad, low, chunks, 0, 1)
    rest = outer_sums(scal, queries, out_grad, low, chunks, 1, chunks - 1)
    own_terms = split_terms([inputs])
    rev0 = scan_states(sums, True)
    rev1 = scan_states(rest, True)
    fwd = scan_states(outer_sums(scal, values, keys, low, chunks, 0, chunks), False)

    eighth, at, far_terms = inputs.shape[1] // 8, 0, []
    for sizes in PIECES:
        pieces = []
        for size in sizes:
            piece = inputs[:, at * eighth : (at + size) * eighth]
            pieces.append(over_seq(piece, low))
            at = at + size
        far_terms.append(split_terms(pieces))

    def state_of(a):
        return (rev0, 0) if a == 0 else (rev1, a - 1)

    gathered = []
    for a in range(chunks):
        grads = value_grads(scal, queries, keys, out_grad, *state_of(a), scale, low, chunks, a)
        if a >= ALONE:
            got = permute(
                grads, lambda s, h: None if ((s // low) & 1) == (h & 1) else (s ^ low, h ^ 1)
            )
            grads = jnp.where(first, grads, got)
        mine, other, bit = [grads], [over_head(grads, 1)], 1
        while bit < ny:
            more = [over_head(x, 2 * bit) for x in mine]
            mine, other = mine + more, other + [over_head(x, 1) for x in more]
            bit *= 2
        gathered.append((mine, other))

    def reduced(added, bit):
        count = added[0].shape[0]
        while count > 1:
            count //= 2
            both = functools.reduce(jnp.add, added)
            added = [both[:count], over_seq(both[count:], bit * count)]
        return added

    cells = []
    for a in range(chunks):
        row, offset = [], 0
        groups = [[x] for x in far_terms] if a in SPLIT else [far_terms]
        for fars in groups:
            size = sum(x[0].shape[1] for x in fars)
            keep, send = weight_parts(
                scal, *gathered[a], own_terms,
                fars if a >= ALONE else [], offset, size,
            )
            offset += size
            parts = [keep, over_seq(send, 1)]
            if a < ALONE:
                parts = [x[0] for x in reduced(parts, low)]
            row.append(reduced(parts, 2 * low))
        cells.append(row)

    grads = ()
    for begin, count in ((0, 1), (1, chunks - 1)):
        rev, at = state_of(begin)
        grads = query_key_grads(
            scal, queries, keys, values, out_grad,
            fwd, rev, at, scale, low, chunks, begin, count, grads,
        )
    update, row_next, col_next = update_block(cells, row_state, col_state, weight_scale)
    return (*grads, update, row_next, col_next)


def solution(mesh):
    tok, rows = P("seq", "head"), P("head", "seq")

    return jax.shard_map(
        shards,
        mesh=mesh,
        in_specs=(tok, tok, tok, tok, tok, rows, tok),
        out_specs=(tok, tok, tok, rows, tok),
        check_vma=False,
    )
```

```python
import functools
import math
import jax
import jax.numpy as jnp
from jax import lax
from jax.experimental import pallas as pl
from jax.experimental.pallas import tpu as pltpu
from jax.sharding import PartitionSpec as P


HEAD_DIM = 128
MOMENT_EPS = 1e-06
DECAY = 0.9
F32 = jnp.float32
BF16 = jnp.bfloat16
AXES = ("seq", "head")
ALONE = 1
PIECES = ((1, 1, 1, 1), (2, 2))
SPLIT = (0, 1, 2, 3)
NN = (((1,), (0,)), ((), ()))
NT = (((1,), (1,)), ((), ()))
TN = (((0,), (0,)), ((), ()))


def split(x):
    hi = x.astype(BF16)
    return hi, (x - hi.astype(F32)).astype(BF16)


def times(a, b, dims):
    return lax.dot_general(a, b, dimension_numbers=dims, preferred_element_type=F32)


def mul_nn(a, b):
    wide = jnp.concatenate(b, axis=1)
    columns = b[0].shape[1]
    if a[0].shape[1] == HEAD_DIM:
        low = jnp.concatenate([b[0], jnp.zeros_like(b[0])], axis=1)
        out = times(jnp.concatenate(a, axis=1), jnp.concatenate([wide, low], axis=0), NN)
        return out[:, :columns] + out[:, columns:]
    out = times(a[0], wide, NN)
    return out[:, :columns] + (out[:, columns:] + times(a[1], b[0], NN))


def mul_nt(a, b):
    both = times(jnp.concatenate(a, axis=1), jnp.concatenate([b[0], b[0]], axis=1), NT)
    return both + times(a[0], b[1], NT)


def mul_tn(a, b):
    columns = b[0].shape[1]
    out = times(a[0], jnp.concatenate(b, axis=1), TN)
    return out[:, :columns] + (out[:, columns:] + times(a[1], b[0], TN))


def params(mib=24):
    return pltpu.CompilerParams(vmem_limit_bytes=mib * 2**20)


def cost(flops, nbytes):
    return pl.CostEstimate(flops=int(flops), bytes_accessed=int(nbytes), transcendentals=0)


def by_phase(phase, count):
    return lambda p, n: jnp.where(p == phase, n, jnp.where(p < phase, 0, count - 1))


def outer_body(low, scal, left, right, *outs):
    out = mul_tn(split(left[...]), split(right[...]))
    for jj in range(low):

        @pl.when(pl.program_id(0) == low - 1 - jj)
        def _():
            outs[jj][0] = out


def outer_sums(scal, left, right, low, chunks, begin, count):
    tokens = left.shape[0]
    spec = pl.BlockSpec(
        (tokens, HEAD_DIM), lambda p, n, s: (0, (s[1] ^ (low - 1 - p)) * chunks + begin + n)
    )

    def out_spec(jj):
        at = by_phase(low - 1 - jj, count)
        return pl.BlockSpec((1, HEAD_DIM, HEAD_DIM), lambda p, n, s: (at(p, n), 0, 0))

    return pl.pallas_call(
        functools.partial(outer_body, low),
        grid_spec=pltpu.PrefetchScalarGridSpec(
            num_scalar_prefetch=1,
            grid=(low, count),
            in_specs=[spec, spec],
            out_specs=[out_spec(jj) for jj in range(low)],
        ),
        out_shape=[jax.ShapeDtypeStruct((count, HEAD_DIM, HEAD_DIM), F32)] * low,
        compiler_params=params(),
        cost_estimate=cost(6 * low * count * tokens * HEAD_DIM**2, 8 * low * count * tokens * HEAD_DIM),
        name="outer_sums",
    )(scal, left, right)


def value_body(scale, blk, scal, q, k, g, mine, other, out):
    count = q.shape[0] // blk
    src = lax.broadcasted_iota(jnp.int32, (blk, blk), 0)
    tgt = lax.broadcasted_iota(jnp.int32, (blk, blk), 1)
    later = jnp.where(pl.program_id(0) == 0, mine[0], other[0])
    for n in reversed(range(count)):
        rows = pl.ds(n * blk, blk)
        qn, kn, gn = split(q[rows, :]), split(k[rows, :]), split(g[rows, :])
        scores = jnp.where(src <= tgt, mul_nt(kn, qn), 0.0)
        grad = mul_nn(split(scores), gn) + mul_nn(kn, split(later))
        out[0, :, rows] = (scale * grad).T
        if n:
            later = later + mul_tn(qn, gn)


def value_grads(scal, q, k, g, state, at, scale, low, chunks, a):
    tokens = q.shape[0]
    blk = min(256, tokens)
    spec = pl.BlockSpec((tokens, HEAD_DIM), lambda j, s: (0, (s[1] ^ j) * chunks + a))
    state_spec = pl.BlockSpec((1, HEAD_DIM, HEAD_DIM), lambda j, s: (at, 0, 0))
    return pl.pallas_call(
        functools.partial(value_body, scale, blk),
        grid_spec=pltpu.PrefetchScalarGridSpec(
            num_scalar_prefetch=1,
            grid=(low,),
            in_specs=[spec, spec, spec, state_spec, state_spec],
            out_specs=pl.BlockSpec((1, HEAD_DIM, tokens), lambda j, s: (s[1] ^ j, 0, 0)),
        ),
        out_shape=jax.ShapeDtypeStruct((low, HEAD_DIM, tokens), F32),
        compiler_params=params(),
        cost_estimate=cost(12 * low * tokens * blk * HEAD_DIM, 16 * low * tokens * HEAD_DIM),
        name="value_grads",
    )(scal, q, k, g, *state)


def query_key_body(scale, blk, scal, q, k, v, g, fwd, fwd_other, rev, rev_other, *refs):
    qg, kg = refs[-2:]
    count = q.shape[0] // blk
    here = pl.program_id(0) == 0
    tgt = lax.broadcasted_iota(jnp.int32, (blk, blk), 0)
    src = lax.broadcasted_iota(jnp.int32, (blk, blk), 1)
    before = [jnp.where(here, fwd[0], fwd_other[0])]
    for n in range(count - 1):
        rows = pl.ds(n * blk, blk)
        before.append(before[-1] + mul_tn(split(v[rows, :]), split(k[rows, :])))
    later = jnp.where(here, rev[0], rev_other[0])
    for n in reversed(range(count)):
        rows = pl.ds(n * blk, blk)
        qn, kn = split(q[rows, :]), split(k[rows, :])
        vn, gn = split(v[rows, :]), split(g[rows, :])
        scores = split(jnp.where(src <= tgt, mul_nt(gn, vn), 0.0))
        qg[rows, :] = scale * (mul_nn(scores, kn) + mul_nn(gn, split(before[n])))
        kg[rows, :] = scale * (mul_tn(scores, qn) + mul_nn(vn, split(later.T)))
        if n:
            later = later + mul_tn(qn, gn)


def query_key_grads(scal, q, k, v, g, fwd, rev, at, scale, low, chunks, a, count, filled):
    tokens, width = q.shape
    blk = min(256, tokens)
    spec = pl.BlockSpec((tokens, HEAD_DIM), lambda j, n, s: (0, (s[1] ^ j) * chunks + a + n))
    fwd_spec = pl.BlockSpec((1, HEAD_DIM, HEAD_DIM), lambda j, n, s: (a + n, 0, 0))
    rev_spec = pl.BlockSpec((1, HEAD_DIM, HEAD_DIM), lambda j, n, s: (at + n, 0, 0))
    kept = [pl.BlockSpec(memory_space=pl.ANY)] * len(filled)
    return pl.pallas_call(
        functools.partial(query_key_body, scale, blk),
        grid_spec=pltpu.PrefetchScalarGridSpec(
            num_scalar_prefetch=1,
            grid=(low, count),
            in_specs=[spec] * 4 + [fwd_spec] * 2 + [rev_spec] * 2 + kept,
            out_specs=[spec, spec],
        ),
        out_shape=[jax.ShapeDtypeStruct((tokens, width), F32)] * 2,
        input_output_aliases={9 + n: n for n in range(len(filled))},
        compiler_params=params(),
        cost_estimate=cost(30 * tokens * blk * low * count * HEAD_DIM, 24 * tokens * low * count * HEAD_DIM),
        name="query_key_grads",
    )(scal, q, k, v, g, *fwd, *rev, *filled)


def terms_body(blk, *refs):
    pieces, (hi, lo) = refs[:-2], refs[-2:]
    at = 0
    for ref in pieces:
        for begin in range(0, ref.shape[1], min(blk, ref.shape[1])):
            size = min(blk, ref.shape[1] - begin)
            where = (at // blk, slice(None), pl.ds(at % blk, size))
            hi[where], lo[where] = split(ref[:, pl.ds(begin, size)])
            at += size


def split_terms(pieces, blk):
    tokens, width = pieces[0].shape[0], sum(x.shape[1] for x in pieces)
    rows = min(256, tokens)
    spec = pl.BlockSpec((width // blk, rows, blk), lambda n: (0, n, 0))
    return pl.pallas_call(
        functools.partial(terms_body, blk),
        grid=(tokens // rows,),
        in_specs=[pl.BlockSpec((rows, x.shape[1]), lambda n: (n, 0)) for x in pieces],
        out_specs=[spec] * 2,
        out_shape=[jax.ShapeDtypeStruct((width // blk, tokens, blk), BF16)] * 2,
        compiler_params=params(),
        cost_estimate=cost(4 * tokens * width, 8 * tokens * width),
        name="split_terms",
    )(*pieces)


def rows_times(blocks, hi, lo):
    parts = [split(x) for x in blocks]
    high = jnp.concatenate([p[0] for p in parts], axis=0)
    both = jnp.concatenate([high] + [p[1] for p in parts], axis=0)
    wide = jnp.dot(both, hi, preferred_element_type=F32)
    rows = high.shape[0]
    return wide[:rows] + (wide[rows:] + jnp.dot(high, lo, preferred_element_type=F32))


def weight_body(ny, low, counts, scal, *refs):
    mine, other = refs[:ny], refs[ny : 2 * ny]
    own_hi, own_lo = refs[2 * ny : 2 * ny + 2]
    far, outs = refs[2 * ny + 2 : -low], refs[-low:]
    first = scal[0] == 1
    a, b = [x[0] for x in mine], [x[0] for x in other]
    if far:
        far_hi, far_lo, at = far[0][0], far[1][0], 0
        for c in range(1, len(counts)):
            at += counts[c - 1]
            later = pl.program_id(1) >= at
            far_hi = jnp.where(later, far[2 * c][0], far_hi)
            far_lo = jnp.where(later, far[2 * c + 1][0], far_lo)
        own_rows = [jnp.where(first, x, y) for x, y in zip(a, b)]
        far_rows = [jnp.where(first, y, x) for x, y in zip(a, b)]
        total = rows_times(own_rows, own_hi[0], own_lo[0]) + rows_times(far_rows, far_hi, far_lo)
        places = [(scal[2] ^ n,) for n in range(ny)]
    else:
        total = rows_times(a + b, own_hi[0], own_lo[0])
        places = [(1 - scal[0], scal[2] ^ n) for n in range(ny)]
        places += [(scal[0], scal[2] ^ n) for n in range(ny)]
    height = total.shape[0] // len(places)
    for jj in range(low):

        @pl.when(pl.program_id(0) == low - 1 - jj)
        def _():
            for n, place in enumerate(places):
                outs[jj][place] = total[n * height : (n + 1) * height]


def weight_parts(scal, mine, other, own, fars, offset, width):
    ny = len(mine)
    low, height, tokens = mine[0].shape
    blk = own[0].shape[2]
    counts = [x[0].shape[0] for x in fars]
    count, first = width // blk, offset // blk
    lead = (ny, height) if fars else (2, ny, height)
    grad_spec = pl.BlockSpec((1, height, tokens), lambda p, n, s: (s[1] ^ (low - 1 - p), 0, 0))
    own_spec = pl.BlockSpec((1, tokens, blk), lambda p, n, s: (n + first, 0, 0))

    def far_spec(c):
        begin = sum(counts[:c])
        return pl.BlockSpec((1, tokens, blk), lambda p, n, s: (jnp.clip(n - begin, 0, counts[c] - 1), 0, 0))

    def out_spec(jj):
        col = by_phase(low - 1 - jj, count)
        zeros = (0,) * len(lead)
        return pl.BlockSpec(lead + (blk,), lambda p, n, s: zeros + (col(p, n),))

    return pl.pallas_call(
        functools.partial(weight_body, ny, low, counts),
        grid_spec=pltpu.PrefetchScalarGridSpec(
            num_scalar_prefetch=1,
            grid=(low, count),
            in_specs=[grad_spec] * (2 * ny)
            + [own_spec] * 2
            + [far_spec(c) for c in range(len(fars)) for _ in range(2)],
            out_specs=[out_spec(jj) for jj in range(low)],
        ),
        out_shape=[jax.ShapeDtypeStruct(lead + (width,), F32)] * low,
        compiler_params=params(),
        cost_estimate=cost(
            12 * ny * low * height * tokens * width,
            8 * ny * low * height * tokens + 8 * tokens * width + 8 * ny * height * width,
        ),
        name="weight_parts",
    )(scal, *mine, *other, *own, *[x for pair in fars for x in pair])


def update_body(scale, counts, row_state, col_state, *refs):
    parts, (update, row_next, col_next) = list(refs[:-3]), refs[-3:]
    height = parts[0].shape[-2]
    rows, columns = update.shape
    row_cols = []
    total = jnp.zeros((1, 1), F32)
    col_next[...] = jnp.zeros_like(col_next)
    for a, cells in enumerate(counts):
        at = pl.ds(a * height, height)
        row_sum, begin = jnp.zeros((height, 1), F32), 0
        for count in cells:
            cols = pl.ds(begin, parts[0].shape[-1])
            begin += parts[0].shape[-1]
            block = parts.pop(0)[0]
            for _ in range(count - 1):
                block = block + parts.pop(0)[0]
            block = block * scale
            update[at, cols] = block
            squares = block * block
            row_sum = row_sum + jnp.sum(squares, axis=1, keepdims=True)
            col_next[:, cols] += jnp.sum(squares, axis=0, keepdims=True)
        mean = row_sum * (1.0 / columns) + MOMENT_EPS
        lanes = jnp.broadcast_to(mean, (height, height)).T[:1]
        nxt = DECAY * row_state[:, at] + (1.0 - DECAY) * lanes
        row_next[:, at] = nxt
        total = total + jnp.sum(nxt, axis=1, keepdims=True)
        row_cols.append(jnp.broadcast_to(nxt, (height, height)).T[:, :1])
    average = total * (1.0 / rows)
    nxt = DECAY * col_state[...] + (1.0 - DECAY) * (col_next[...] * (1.0 / rows) + MOMENT_EPS)
    col_next[...] = nxt
    for a in range(len(counts)):
        at = pl.ds(a * height, height)
        update[at, :] = update[at, :] / jnp.sqrt(row_cols[a] * nxt / average)


def update_block(parts, row_state, col_state, scale):
    chunks = len(parts)
    counts = tuple(tuple(len(cell) for cell in row) for row in parts)
    flat = [x for row in parts for cell in row for x in cell]
    height = flat[0].shape[-2]
    cell = lambda x: pl.BlockSpec((1,) + x.shape[-2:], lambda n: (0, 0, 0))
    full = lambda x: pl.BlockSpec(x.shape, lambda n: (0, 0))
    shape = (chunks * height, col_state.shape[1])
    out_shape = [
        jax.ShapeDtypeStruct(shape, F32),
        jax.ShapeDtypeStruct(row_state.shape, F32),
        jax.ShapeDtypeStruct(col_state.shape, F32),
    ]
    return pl.pallas_call(
        functools.partial(update_body, scale, counts),
        grid=(1,),
        in_specs=[full(row_state), full(col_state)] + [cell(x) for x in flat],
        out_specs=[full(x) for x in out_shape],
        out_shape=out_shape,
        compiler_params=params(),
        cost_estimate=cost(20 * shape[0] * shape[1], 16 * shape[0] * shape[1]),
        name="update_block",
    )(row_state, col_state, *flat)


def shards(queries, keys, values, out_grad, inputs, row_state, col_state):
    tokens, width = queries.shape
    n_seq, n_head = lax.axis_size("seq"), lax.axis_size("head")
    heads = width // HEAD_DIM
    low = n_seq // n_head
    ny = n_head // 2
    chunks = heads // low
    scale = 1.0 / float(HEAD_DIM * tokens * n_seq) ** 0.5
    weight_scale = 1.0 / float(tokens * n_seq) ** 0.5
    assert low == 2 and chunks > 1

    def permute(x, go):
        pairs = []
        for s in range(n_seq):
            for h in range(n_head):
                to = go(s, h)
                if to is not None:
                    pairs.append((s * n_head + h, to[0] * n_head + to[1]))
        return lax.ppermute(x, AXES, pairs)

    def over_seq(x, bit):
        return permute(x, lambda s, h: (s ^ bit, h))

    def over_head(x, bit):
        return permute(x, lambda s, h: (s, h ^ bit))

    seq, head = lax.axis_index("seq"), lax.axis_index("head")
    plane = (seq // low) & 1
    first = plane == (head & 1)
    part = seq % low
    scal = jnp.stack([first.astype(jnp.int32), part, (head // 2) ^ (seq // (2 * low))]).astype(jnp.int32)

    def scan_states(sums, reverse):
        keep, send = sums
        got = over_seq(send, 1)
        total, enter, bit = keep + got, jnp.zeros_like(keep), low
        while bit < n_seq:
            wanted = lambda s: 2 * bit < n_seq or bool(s & bit) == reverse
            came = permute(total, lambda s, h: (s ^ bit, h) if wanted(s) else None)
            take = ((seq & bit) == 0) if reverse else ((seq & bit) != 0)
            enter = enter + jnp.where(take, came, 0.0)
            bit *= 2
            if bit < n_seq:
                total = total + came
        last = 0 if reverse else 1
        mine = enter + jnp.where(part == last, got, 0.0)
        out = enter + jnp.where(part == last, 0.0, keep)
        return mine, over_seq(out, 1)

    sums = outer_sums(scal, queries, out_grad, low, chunks, 0, 1)
    rest = outer_sums(scal, queries, out_grad, low, chunks, 1, chunks - 1)
    parts = [sum(sizes) * inputs.shape[1] // 8 for sizes in PIECES]
    blk = math.gcd(256, *parts)
    own_terms = split_terms([inputs], blk)
    rev0 = scan_states(sums, True)
    rev1 = scan_states(rest, True)
    fwd = scan_states(outer_sums(scal, values, keys, low, chunks, 0, chunks), False)

    eighth, at, far_terms = inputs.shape[1] // 8, 0, []
    for sizes in PIECES:
        pieces = []
        for size in sizes:
            piece = inputs[:, at * eighth : (at + size) * eighth]
            pieces.append(over_seq(piece, low))
            at = at + size
        far_terms.append(split_terms(pieces, blk))

    def state_of(a):
        return (rev0, 0) if a == 0 else (rev1, a - 1)

    gathered = []
    for a in range(chunks):
        grads = value_grads(scal, queries, keys, out_grad, *state_of(a), scale, low, chunks, a)
        if a >= ALONE:
            got = permute(
                grads, lambda s, h: None if ((s // low) & 1) == (h & 1) else (s ^ low, h ^ 1)
            )
            grads = jnp.where(first, grads, got)
        mine, other, bit = [grads], [over_head(grads, 1)], 1
        while bit < ny:
            more = [over_head(x, 2 * bit) for x in mine]
            mine, other = mine + more, other + [over_head(x, 1) for x in more]
            bit *= 2
        gathered.append((mine, other))

    def reduced(added, bit):
        count = added[0].shape[0]
        while count > 1:
            count //= 2
            both = functools.reduce(jnp.add, added)
            added = [both[:count], over_seq(both[count:], bit * count)]
        return added

    cells = []
    for a in range(chunks):
        row, offset = [], 0
        groups = [[x] for x in far_terms] if a in SPLIT else [far_terms]
        for fars in groups:
            size = blk * sum(x[0].shape[0] for x in fars)
            keep, send = weight_parts(
                scal, *gathered[a], own_terms,
                fars if a >= ALONE else [], offset, size,
            )
            offset += size
            parts = [keep, over_seq(send, 1)]
            if a < ALONE:
                parts = [x[0] for x in reduced(parts, low)]
            row.append(reduced(parts, 2 * low))
        cells.append(row)

    grads = ()
    for begin, count in ((0, 1), (1, chunks - 1)):
        rev, at = state_of(begin)
        grads = query_key_grads(
            scal, queries, keys, values, out_grad,
            fwd, rev, at, scale, low, chunks, begin, count, grads,
        )
    update, row_next, col_next = update_block(cells, row_state, col_state, weight_scale)
    return (*grads, update, row_next, col_next)


def solution(mesh):
    tok, rows = P("seq", "head"), P("head", "seq")

    return jax.shard_map(
        shards,
        mesh=mesh,
        in_specs=(tok, tok, tok, tok, tok, rows, tok),
        out_specs=(tok, tok, tok, rows, tok),
        check_vma=False,
    )
```
